128 devices in a mesh: row: 16 (over x, z), col: 8 (over y, core).
Axes of the slice: x: 4, y: 4, z: 4, core: 2. Of those that a mesh axis runs over, the one named last changes fastest.
Arguments:
- teacher_rows: bfloat16 [256, 8192], P('col', 'row'), may hold values from -6 to 6
- projection: bfloat16 [8192, 4608], P('row'), may hold values from -0.0625 to 0.0625
- student_in: bfloat16 [256, 4608], P('col', 'row'), may hold values from -36 to 36, as said below
- norm_gain: bfloat16 [4608], P('row'), may hold values from 0.5 to 1.5
- w_gate: bfloat16 [4608, 36864], P('row', 'col'), may hold values from -0.09375 to 0.09375
- w_up: bfloat16 [4608, 36864], P('row', 'col'), may hold values from -0.09375 to 0.09375
- w_down: bfloat16 [4608, 36864], P('row', 'col'), may hold values from -0.03125 to 0.03125
- row_old: float32 [3, 4608], P(None, 'row'), may hold values from 1.953125e-05 to 0.001953125
- col_old: float32 [3, 36864], P(None, 'col'), may hold values from 1.953125e-05 to 0.001953125
Outputs:
- update_gate: bfloat16 [4608, 36864], P('row', 'col')
- update_up: bfloat16 [4608, 36864], P('row', 'col')
- update_down: bfloat16 [4608, 36864], P('row', 'col')
- row_factors: float32 [3, 4608], P(None, 'row')
- col_factors: float32 [3, 36864], P(None, 'col')
- distill_loss: float32 [], replicated
The draws below stay inside these ranges and needn't reach their ends.
Inputs may be any that keep to these rules, and one draw needn't show every extreme that they name: `student_in`: student hidden rows of varying magnitude.
All inputs are finite; a program needn't handle non-finite values.
Results may differ from the reference program's by a relative error of at most 0.0075.
Values may be sent and summed in bfloat16 or wider, within the bound.
A program may use at most 128 MiB of HBM per device.

```python
import math
import jax
import jax.numpy as jnp
from jax import lax

D = 4608
FF = 36864
KT = 8192
TOKENS = 256


def draw_student_in(key, part):
    noise_key, group_key, region_key, sign_key, size_key = jax.random.split(key, 5)
    values = jnp.clip(jax.random.normal(noise_key, (TOKENS, D), jnp.float32), -6.0, 6.0)
    feat_pos = jnp.arange(D, dtype=jnp.float32) / D
    tok_pos = jnp.arange(TOKENS, dtype=jnp.float32) / TOKENS
    in_group = jnp.where(jax.random.uniform(group_key, (TOKENS,), jnp.float32) < 0.5, 1.0, 0.0)
    in_region = jnp.where(jax.random.uniform(region_key, (D,), jnp.float32) < 0.5, 1.0, 0.0)
    sign_flip = jnp.where(jax.random.uniform(sign_key, (D,), jnp.float32) < 0.5, -1.0, 1.0)
    shared_size = jax.random.uniform(size_key, (D,), jnp.float32, 0.5, 1.5)
    feat_scale = 1.0 + feat_pos
    tok_scale = 1.0 + 0.7 * tok_pos
    strength = 2.5
    shared_part = strength * in_region * sign_flip * shared_size
    combined = values * tok_scale[:, None] * feat_scale[None, :] + in_group[:, None] * shared_part[None, :]
    return jnp.clip(combined, -36.0, 36.0).astype(jnp.bfloat16)


def level_of(own_key, extent, pieces, least, high):
    level = 1.0
    for axis_at, shards_of in pieces:
        steps = jax.random.uniform(jax.random.fold_in(jax.random.fold_in(own_key, 6), axis_at), (shards_of,), jnp.float32, least / len(pieces), high / len(pieces))
        level = level * jnp.repeat(jnp.exp(steps), extent[axis_at] // shards_of).reshape((-1,) + (1,) * (len(extent) - 1 - axis_at))
    return level


def scatter_about(rng, extent, deviation, bound, shards=(), kind=jnp.bfloat16):
    drawn = jax.random.normal(rng, extent, jnp.float32) * deviation
    if len(shards) > 0:
        drawn = level_of(rng, extent, shards, -0.22, 0.18) * drawn
    return jnp.clip(drawn, min=-bound, max=bound).astype(kind)


def setup_inputs(seed: int = 0) -> dict:
    seeds = jax.random.split(jax.random.key(seed), 10)
    return {
        "teacher_rows": scatter_about(seeds[0], (TOKENS, KT), 1.0, 6.0, ((0, 8), (1, 16))),
        "projection": scatter_about(seeds[1], (KT, D), KT ** -0.5, 0.0625, ((0, 16),)),
        "student_in": draw_student_in(jax.random.fold_in(seeds[9], 71), 0),
        "norm_gain": jnp.clip(1.0 + 0.1 * jax.random.normal(seeds[3], (D,), jnp.float32), 0.5, 1.5).astype(jnp.bfloat16),
        "w_gate": scatter_about(seeds[4], (D, FF), D ** -0.5, 0.09375, ((0, 16), (1, 8))),
        "w_up": scatter_about(seeds[5], (D, FF), D ** -0.5, 0.09375, ((0, 16), (1, 8))),
        "w_down": scatter_about(seeds[6], (D, FF), FF ** -0.5, 0.03125, ((0, 16), (1, 8))),
        "row_old": jnp.clip(jnp.exp(math.log(0.001953125) - 4.6051702 * jax.random.uniform(seeds[7], (3, D), jnp.float32) ** level_of(seeds[7], (3, D), ((1, 16),), -0.2, 0.2)), 1.9531249563442543e-05, 0.001953125),
        "col_old": jnp.clip(jnp.exp(math.log(0.001953125) - 4.6051702 * jax.random.uniform(seeds[8], (3, FF), jnp.float32) ** level_of(seeds[8], (3, FF), ((1, 8),), -0.2, 0.2)), 1.9531249563442543e-05, 0.001953125),
    }


def gelu_pair(values):
    root_coef = math.sqrt(2.0 / math.pi)
    tangent = jnp.tanh(root_coef * (values + 0.044715 * values * values * values))
    gelu_val = 0.5 * values * (1.0 + tangent)
    gelu_slope = 0.5 * (1.0 + tangent) + 0.5 * values * (1.0 - tangent * tangent) * root_coef * (1.0 + 3.0 * 0.044715 * values * values)
    return (gelu_val, gelu_slope)

def factored(gradient, row_prev, col_prev):
    decay_rate = 0.8
    squares = gradient * gradient + 1e-30
    row_new = decay_rate * row_prev + (1.0 - decay_rate) * lax.optimization_barrier(jnp.sum(squares, axis=1)) / FF
    col_new = decay_rate * col_prev + (1.0 - decay_rate) * lax.optimization_barrier(jnp.sum(squares, axis=0)) / D
    updates = gradient / jnp.sqrt(row_new[:, None] * col_new[None, :])
    update_rms = jnp.sqrt(jnp.sum(updates * updates) / (D * FF))
    return ((updates / jnp.maximum(1.0, update_rms)).astype(jnp.bfloat16), row_new, col_new)

def reference(teacher_rows, projection, student_in, norm_gain, w_gate, w_up, w_down, row_old, col_old):
    target = jnp.dot(teacher_rows, projection, preferred_element_type=jnp.float32).astype(jnp.bfloat16)
    inputs = student_in.astype(jnp.float32)
    mean_sq = lax.optimization_barrier(jnp.mean(inputs * inputs, axis=1, keepdims=True))
    inv_rms = 1.0 / jnp.sqrt(mean_sq + 1e-06)
    normed = (inputs * inv_rms * norm_gain.astype(jnp.float32)[None, :]).astype(jnp.bfloat16)
    gate_sum = jnp.dot(normed, w_gate, preferred_element_type=jnp.float32)
    up_sum = jnp.dot(normed, w_up, preferred_element_type=jnp.float32)
    gelu_val, gelu_slope = gelu_pair(gate_sum)
    hidden = (gelu_val * up_sum).astype(jnp.bfloat16)
    down_out = lax.dot_general(hidden, w_down, (((1,), (1,)), ((), ())), preferred_element_type=jnp.float32)
    residue = inputs + down_out - target.astype(jnp.float32)
    loss_total = 0.5 * jnp.sum(residue * residue) / TOKENS
    grad_out = (residue / TOKENS).astype(jnp.bfloat16)
    grad_down = lax.dot_general(grad_out, hidden, (((0,), (0,)), ((), ())), preferred_element_type=jnp.float32)
    grad_hidden = jnp.dot(grad_out, w_down, preferred_element_type=jnp.float32)
    grad_gatein = (grad_hidden * up_sum * gelu_slope).astype(jnp.bfloat16)
    grad_upin = (grad_hidden * gelu_val).astype(jnp.bfloat16)
    grad_gate = lax.dot_general(normed, grad_gatein, (((0,), (0,)), ((), ())), preferred_element_type=jnp.float32)
    grad_up = lax.dot_general(normed, grad_upin, (((0,), (0,)), ((), ())), preferred_element_type=jnp.float32)
    update_gate, row_gate, col_gate = factored(grad_gate, row_old[0], col_old[0])
    update_up, row_up, col_up = factored(grad_up, row_old[1], col_old[1])
    update_down, row_down, col_down = factored(grad_down, row_old[2], col_old[2])
    row_factors = jnp.stack([row_gate, row_up, row_down])
    col_factors = jnp.stack([col_gate, col_up, col_down])
    return (update_gate, update_up, update_down, row_factors, col_factors, loss_total)
```

```python
import math

import jax
import jax.numpy as jnp
from jax import lax
from jax.experimental import pallas as pl
from jax.experimental.pallas import tpu as pltpu
from jax.sharding import PartitionSpec as P

D = 4608
FF = 36864
TOKENS = 256
NR = 16
NC = 8
DL = D // NR
FL = FF // NC
FH = FL // 2
TL = TOKENS // NC
TILE = 768
F32 = jnp.float32
BF16 = jnp.bfloat16
VMEM_LIMIT = 62 * 1024 * 1024


def gelu_pair(values):
    root_coef = math.sqrt(2.0 / math.pi)
    tangent = jnp.tanh(root_coef * (values + 0.044715 * values * values * values))
    gelu_val = 0.5 * values * (1.0 + tangent)
    gelu_slope = 0.5 * (1.0 + tangent) + 0.5 * values * (1.0 - tangent * tangent) * root_coef * (
        1.0 + 3.0 * 0.044715 * values * values
    )
    return (gelu_val, gelu_slope)


def remote(src, dst, send_sem, recv_sem, axis, index):
    return pltpu.make_async_remote_copy(
        src_ref=src,
        dst_ref=dst,
        send_sem=send_sem,
        recv_sem=recv_sem,
        device_id={axis: index},
        device_id_type=pl.DeviceIdType.MESH,
    )


def enter(me, c):
    barrier = pltpu.get_barrier_semaphore()
    for d in range(1, NR):
        pl.semaphore_signal(
            barrier, inc=1, device_id={"row": lax.rem(me + d, NR)},
            device_id_type=pl.DeviceIdType.MESH,
        )
    for d in range(1, NC):
        pl.semaphore_signal(
            barrier, inc=1, device_id={"col": lax.rem(c + d, NC)},
            device_id_type=pl.DeviceIdType.MESH,
        )
    pl.semaphore_wait(barrier, NR + NC - 2)


def exchange(axis, me, n, source, slots, send_sem, recv_sem):
    copies = []
    for d in range(1, n):
        peer = lax.rem(me + d, n)
        copy = remote(
            source(peer), slots(d), send_sem.at[d - 1], recv_sem.at[d - 1], axis, peer
        )
        copy.start()
        copies.append(copy)
    return copies


def finish(copies):
    for copy in copies:
        copy.wait_recv()
    for copy in copies:
        copy.wait_send()


class Scatter:
    def __init__(self, buf, rows, lo, width, p, plus, minus, recv, acc, ss, rs):
        self.buf, self.rows, self.lo, self.half = buf, rows, lo, width // 2
        self.p, self.plus, self.minus = p, plus, minus
        self.recv, self.acc, self.ss, self.rs = recv, acc, ss, rs

    def part(self, k, which):
        at = pl.multiple_of(lax.rem(self.p + k, 4) * self.rows, 16)
        return self.buf.at[pl.ds(at, self.rows), pl.ds(self.lo + which * self.half, self.half)]

    def send(self, src, slot, to):
        copy = remote(
            src, self.recv.at[slot], self.ss.at[slot], self.rs.at[slot], "row", to
        )
        copy.start()
        return copy

    def start(self):
        self.copies = [
            self.send(self.part(2, 0), 0, self.plus),
            self.send(self.part(2, 1), 1, self.minus),
            self.send(self.part(1, 1), 2, self.plus),
            self.send(self.part(3, 0), 3, self.minus),
        ]

    def relay(self):
        self.copies[0].wait_recv()
        self.acc[0] = (self.part(1, 0)[...].astype(F32) + self.recv[0].astype(F32)).astype(BF16)
        self.copies.append(self.send(self.acc.at[0], 4, self.plus))
        self.copies[1].wait_recv()
        self.acc[1] = (self.part(3, 1)[...].astype(F32) + self.recv[1].astype(F32)).astype(BF16)
        self.copies.append(self.send(self.acc.at[1], 5, self.minus))

    def result(self):
        for at in (3, 2, 4, 5):
            self.copies[at].wait_recv()
        first = self.part(0, 0)[...].astype(F32) + self.recv[3].astype(F32) + self.recv[4].astype(F32)
        second = self.part(0, 1)[...].astype(F32) + self.recv[2].astype(F32) + self.recv[5].astype(F32)
        return (first, second)

    def drain(self):
        for copy in self.copies:
            copy.wait_send()


class Gather:
    def __init__(self, buf, base, rows, lo, width, p, plus, minus, ss, rs):
        self.buf, self.base, self.rows, self.lo, self.width = buf, base, rows, lo, width
        self.p, self.plus, self.minus, self.ss, self.rs = p, plus, minus, ss, rs

    def part(self, k, lo, width):
        at = pl.multiple_of(self.base + lax.rem(self.p + k, 4) * self.rows, 16)
        return self.buf.at[pl.ds(at, self.rows), pl.ds(self.lo + lo, width)]

    def send(self, ref, slot, to):
        copy = remote(ref, ref, self.ss.at[slot], self.rs.at[slot], "row", to)
        copy.start()
        return copy

    def start(self):
        self.copies = [
            self.send(self.part(0, 0, self.width), 0, self.plus),
            self.send(self.part(0, 0, self.width), 1, self.minus),
        ]

    def relay(self):
        half = self.width // 2
        self.copies[0].wait_recv()
        self.copies.append(self.send(self.part(3, 0, half), 2, self.plus))
        self.copies[1].wait_recv()
        self.copies.append(self.send(self.part(1, half, half), 3, self.minus))

    def done(self):
        self.copies[2].wait_recv()
        self.copies[3].wait_recv()

    def drain(self):
        for copy in self.copies:
            copy.wait_send()


def eye(rows, lanes):
    return lax.broadcasted_iota(jnp.int32, (rows, lanes), 0) == lax.broadcasted_iota(
        jnp.int32, (rows, lanes), 1
    )


def step_kernel(
    teacher, projection, student, gain, w_gate, w_up, w_down,
    normed_out, dy_out, hidden_out, grads_out, loss_out,
    proj_v, wg_v, wu_v, wd_v, sq, sq_in, tpart, tpart_in, normed, part, mid, recv1, acc1,
    recv2, acc2, hidden, act_v, ups_v, down_acc, down_part, down_in, dy, gpart, gmid,
    grecv1, gacc1, grecv2, gacc2, grads,
    load_sem, out_sem, sq_ss, sq_rs, t_ss, t_rs, n_ss, n_rs, d_ss, d_rs, y_ss, y_rs,
    s_ss, s_rs, g_ss, g_rs,
):
    me = lax.axis_index("row")
    c = lax.axis_index("col")
    x, z = lax.div(me, 4), lax.rem(me, 4)
    loads = [
        pltpu.make_async_copy(src, dst, load_sem.at[i])
        for i, (src, dst) in enumerate(
            ((projection, proj_v), (w_gate, wg_v), (w_up, wu_v), (w_down, wd_v))
        )
    ]
    for load in loads:
        load.start()
    own = pl.ds(pl.multiple_of(c * TL, TL), TL)
    inputs = student[...].astype(F32)
    diag = eye(TL, 128)
    sums = jnp.sum(inputs * inputs, axis=1, keepdims=True)
    sq[...] = jnp.broadcast_to(
        jnp.sum(jnp.where(diag, sums, 0.0), axis=0, keepdims=True), (8, 128)
    )
    enter(me, c)
    sq_copies = exchange(
        "row", me, NR, lambda peer: sq, lambda d: sq_in.at[d - 1], sq_ss, sq_rs
    )
    loads[0].wait()
    for i in range(4):
        product = jnp.dot(
            teacher[...], proj_v[:, i * 4 * DL : (i + 1) * 4 * DL], preferred_element_type=F32
        )
        for j in range(4):
            tpart[i * 4 + j] = product[:, j * DL : (j + 1) * DL].astype(BF16)
    t_copies = exchange(
        "row", me, NR, lambda peer: tpart.at[peer], lambda d: tpart_in.at[d - 1], t_ss, t_rs
    )
    for copy in sq_copies:
        copy.wait_recv()
    total = sq[0:1] + jnp.sum(sq_in[:, 0, :], axis=0, keepdims=True)
    mean_sq = jnp.sum(jnp.where(diag, total, 0.0), axis=1, keepdims=True) / D
    inv_rms = 1.0 / jnp.sqrt(mean_sq + 1e-06)
    normed[own, :] = (inputs * inv_rms * gain[...].astype(F32)).astype(BF16)
    n_copies = exchange(
        "col", c, NC, lambda peer: normed.at[own, :], lambda d: normed.at[own, :], n_ss, n_rs
    )
    for copy in n_copies:
        copy.wait_recv()
    loads[1].wait()
    loads[2].wait()

    xp, xm = lax.rem(x + 1, 4) * 4 + z, lax.rem(x + 3, 4) * 4 + z
    zp, zm = x * 4 + lax.rem(z + 1, 4), x * 4 + lax.rem(z + 3, 4)
    first = ((x, xp, xm), (z, zp, zm))
    second = ((z, zp, zm), (x, xp, xm))
    scatter1 = [
        Scatter(part, 64, s * FL, FL, *first[s], recv1.at[s], acc1.at[s], s_ss.at[s], s_rs.at[s])
        for s in range(2)
    ]
    scatter2 = [
        Scatter(
            mid.at[s], 16, 0, FL, *second[s], recv2.at[s], acc2.at[s],
            s_ss.at[2 + s], s_rs.at[2 + s],
        )
        for s in range(2)
    ]
    for s in range(2):
        @pl.loop(0, FH // TILE)
        def _(i):
            source = pl.ds(pl.multiple_of(s * FH + i * TILE, 128), TILE)
            to_gate = pl.ds(pl.multiple_of(s * FL + i * TILE, 128), TILE)
            to_up = pl.ds(pl.multiple_of(s * FL + FH + i * TILE, 128), TILE)
            rows = normed[...]
            part[:, to_gate] = jnp.dot(
                rows, wg_v[:, source], preferred_element_type=F32
            ).astype(BF16)
            part[:, to_up] = jnp.dot(
                rows, wu_v[:, source], preferred_element_type=F32
            ).astype(BF16)
        scatter1[s].start()
    for s in range(2):
        scatter1[s].relay()
    for s in range(2):
        a, b = scatter1[s].result()
        mid[s, :, 0:FH] = a.astype(BF16)
        mid[s, :, FH:FL] = b.astype(BF16)
        scatter2[s].start()
    for s in range(2):
        scatter2[s].relay()
    gather1, gather2 = [], []
    for s in range(2):
        gate, up = scatter2[s].result()
        act, slope = gelu_pair(gate)
        act_v[s] = act
        ups_v[s] = up * slope
        p1, p2 = first[s], second[s]
        base = pl.multiple_of(p1[0] * 64, 64)
        at = pl.multiple_of(base + p2[0] * 16, 16)
        hidden[pl.ds(at, 16), s * FH : (s + 1) * FH] = (act * up).astype(BF16)
        gather1.append(
            Gather(hidden, base, 16, s * FH, FH, *p2, g_ss.at[s], g_rs.at[s])
        )
        gather2.append(
            Gather(hidden, 0, 64, s * FH, FH, *p1, g_ss.at[2 + s], g_rs.at[2 + s])
        )
        gather1[s].start()
    for s in range(2):
        gather1[s].relay()
    for s in range(2):
        gather1[s].done()
        gather2[s].start()
    for s in range(2):
        gather2[s].relay()
    finish(t_copies)
    target = tpart[me].astype(F32)
    for d in range(NR - 1):
        target = target + tpart_in[d].astype(F32)
    target = target.astype(BF16).astype(F32)
    loads[3].wait()
    for s in range(2):
        gather2[s].done()
    hidden_copy = pltpu.make_async_copy(hidden, hidden_out, out_sem.at[0])
    hidden_copy.start()
    normed_copy = pltpu.make_async_copy(normed, normed_out, out_sem.at[1])
    normed_copy.start()

    down_acc[...] = jnp.zeros_like(down_acc)

    @pl.loop(0, FL // TILE)
    def _(i):
        lanes = pl.ds(pl.multiple_of(i * TILE, 128), TILE)
        down_acc[...] += lax.dot_general(
            hidden[:, lanes], wd_v[:, lanes], (((1,), (1,)), ((), ())),
            preferred_element_type=F32,
        )

    down_part[...] = down_acc[...].astype(BF16)
    d_copies = exchange(
        "col", c, NC,
        lambda peer: down_part.at[pl.ds(pl.multiple_of(peer * TL, TL), TL), :],
        lambda d: down_in.at[d - 1], d_ss, d_rs,
    )
    for copy in d_copies:
        copy.wait_recv()
    down = down_acc[own, :]
    for d in range(NC - 1):
        down = down + down_in[d].astype(F32)
    residue = inputs + down - target
    loss = jnp.sum(residue * residue)
    loss_out[...] = jnp.zeros_like(loss_out) + loss
    dy[own, :] = (residue / TOKENS).astype(BF16)
    y_copies = exchange(
        "col", c, NC, lambda peer: dy.at[own, :], lambda d: dy.at[own, :], y_ss, y_rs
    )
    for copy in y_copies:
        copy.wait_recv()
    dy_copy = pltpu.make_async_copy(dy, dy_out, out_sem.at[2])
    dy_copy.start()

    gscatter1 = [
        Scatter(
            gpart, 64, s * FH, FH, *first[s], grecv1.at[s], gacc1.at[s],
            s_ss.at[4 + s], s_rs.at[4 + s],
        )
        for s in range(2)
    ]
    gscatter2 = [
        Scatter(
            gmid.at[s], 16, 0, FH, *second[s], grecv2.at[s], gacc2.at[s],
            s_ss.at[6 + s], s_rs.at[6 + s],
        )
        for s in range(2)
    ]
    for s in range(2):
        @pl.loop(0, FH // TILE)
        def _(i):
            lanes = pl.ds(pl.multiple_of(s * FH + i * TILE, 128), TILE)
            gpart[:, lanes] = jnp.dot(
                dy[...], wd_v[:, lanes], preferred_element_type=F32
            ).astype(BF16)
        gscatter1[s].start()
    for s in range(2):
        gscatter1[s].relay()
    for s in range(2):
        a, b = gscatter1[s].result()
        gmid[s, :, 0 : FH // 2] = a.astype(BF16)
        gmid[s, :, FH // 2 : FH] = b.astype(BF16)
        gscatter2[s].start()
    for s in range(2):
        gscatter2[s].relay()
    ggather1, ggather2 = [], []
    for s in range(2):
        halves = gscatter2[s].result()
        p1, p2 = first[s], second[s]
        base = pl.multiple_of(p1[0] * 64, 64)
        at = pl.ds(pl.multiple_of(base + p2[0] * 16, 16), 16)
        for h in range(2):
            lo = h * (FH // 2)
            hi = lo + FH // 2
            grads[at, s * FL + lo : s * FL + hi] = (halves[h] * ups_v[s, :, lo:hi]).astype(BF16)
            grads[at, s * FL + FH + lo : s * FL + FH + hi] = (
                halves[h] * act_v[s, :, lo:hi]
            ).astype(BF16)
        ggather1.append(
            Gather(grads, base, 16, s * FL, FL, *p2, g_ss.at[4 + s], g_rs.at[4 + s])
        )
        ggather2.append(
            Gather(grads, 0, 64, s * FL, FL, *p1, g_ss.at[6 + s], g_rs.at[6 + s])
        )
        ggather1[s].start()
    for s in range(2):
        ggather1[s].relay()
    for s in range(2):
        ggather1[s].done()
        ggather2[s].start()
    for s in range(2):
        ggather2[s].relay()
    for s in range(2):
        ggather2[s].done()
    grads_copy = pltpu.make_async_copy(grads, grads_out, out_sem.at[3])
    grads_copy.start()
    for copy in sq_copies + n_copies + d_copies + y_copies:
        copy.wait_send()
    for group in (scatter1, scatter2, gscatter1, gscatter2, gather1, gather2, ggather1, ggather2):
        for one in group:
            one.drain()
    for copy in (hidden_copy, normed_copy, dy_copy, grads_copy):
        copy.wait()


def whole(space=pltpu.VMEM):
    return pl.BlockSpec(memory_space=space)


def step(teacher, projection, student, gain, w_gate, w_up, w_down):
    sem = pltpu.SemaphoreType.DMA
    q = FH // 2
    return pl.pallas_call(
        step_kernel,
        out_shape=(
            jax.ShapeDtypeStruct((TOKENS, DL), BF16),
            jax.ShapeDtypeStruct((TOKENS, DL), BF16),
            jax.ShapeDtypeStruct((TOKENS, FL), BF16),
            jax.ShapeDtypeStruct((TOKENS, 2 * FL), BF16),
            jax.ShapeDtypeStruct((8, 128), F32),
        ),
        in_specs=[
            whole(), whole(pl.ANY), whole(), whole(), whole(pl.ANY), whole(pl.ANY), whole(pl.ANY)
        ],
        out_specs=(whole(pl.ANY), whole(pl.ANY), whole(pl.ANY), whole(pl.ANY), whole()),
        scratch_shapes=[
            pltpu.VMEM(projection.shape, BF16),
            pltpu.VMEM((DL, FL), BF16),
            pltpu.VMEM((DL, FL), BF16),
            pltpu.VMEM((DL, FL), BF16),
            pltpu.VMEM((8, 128), F32),
            pltpu.VMEM((NR - 1, 8, 128), F32),
            pltpu.VMEM((NR, TL, DL), BF16),
            pltpu.VMEM((NR - 1, TL, DL), BF16),
            pltpu.VMEM((TOKENS, DL), BF16),
            pltpu.VMEM((TOKENS, 2 * FL), BF16),
            pltpu.VMEM((2, 64, FL), BF16),
            pltpu.VMEM((2, 6, 64, FH), BF16),
            pltpu.VMEM((2, 2, 64, FH), BF16),
            pltpu.VMEM((2, 6, 16, FH), BF16),
            pltpu.VMEM((2, 2, 16, FH), BF16),
            pltpu.VMEM((TOKENS, FL), BF16),
            pltpu.VMEM((2, 16, FH), F32),
            pltpu.VMEM((2, 16, FH), F32),
            pltpu.VMEM((TOKENS, DL), F32),
            pltpu.VMEM((TOKENS, DL), BF16),
            pltpu.VMEM((NC - 1, TL, DL), BF16),
            pltpu.VMEM((TOKENS, DL), BF16),
            pltpu.VMEM((TOKENS, FL), BF16),
            pltpu.VMEM((2, 64, FH), BF16),
            pltpu.VMEM((2, 6, 64, q), BF16),
            pltpu.VMEM((2, 2, 64, q), BF16),
            pltpu.VMEM((2, 6, 16, q), BF16),
            pltpu.VMEM((2, 2, 16, q), BF16),
            pltpu.VMEM((TOKENS, 2 * FL), BF16),
            sem((4,)), sem((4,)),
            sem((NR - 1,)), sem((NR - 1,)), sem((NR - 1,)), sem((NR - 1,)),
            sem((NC - 1,)), sem((NC - 1,)), sem((NC - 1,)), sem((NC - 1,)),
            sem((NC - 1,)), sem((NC - 1,)),
            sem((8, 6)), sem((8, 6)), sem((8, 4)), sem((8, 4)),
        ],
        compiler_params=pltpu.CompilerParams(
            collective_id=0, has_side_effects=True, vmem_limit_bytes=VMEM_LIMIT
        ),
        name="step",
    )(teacher, projection, student, gain, w_gate, w_up, w_down)


def stats_kernel(
    normed, dy, hidden, grads, row_old, col_old, loss_in,
    row_out, col_out, total_out,
    left, values, racc, csend, cin, cfull, rsend, rin, cflat, cinv, qsend, qin, qmid, qmid_in,
    c_ss, c_rs, a_ss, a_rs, r_ss, r_rs, q_ss, q_rs, l_ss, l_rs,
):
    me = lax.axis_index("row")
    c = lax.axis_index("col")
    tiles = FL // TILE
    rows_per = TILE // 128
    csend[...] = jnp.zeros_like(csend)
    racc[...] = jnp.zeros_like(racc)
    left[0] = normed[...].astype(F32).T.astype(BF16)
    left[1] = dy[...].astype(F32).T.astype(BF16)

    def tile(m, i):
        lanes = pl.ds(pl.multiple_of(i * TILE, 128), TILE)
        if m == 2:
            return lanes, left[1], hidden[:, lanes]
        at = i * TILE + m * FH + lax.div(i, tiles // 2) * FH
        return lanes, left[0], grads[:, pl.ds(pl.multiple_of(at, 128), TILE)]

    for m in range(3):
        @pl.loop(0, tiles)
        def _(i):
            lanes, lhs, rhs = tile(m, i)
            grad = jnp.dot(lhs, rhs, preferred_element_type=F32)
            values[m, :, lanes] = grad
            square = grad * grad
            folded = square[:, 0:128]
            for k in range(1, rows_per):
                folded = folded + square[:, k * 128 : (k + 1) * 128]
            racc[m] += folded
            down = jnp.sum(square, axis=0, keepdims=True)
            for k in range(rows_per):
                csend[pl.ds(m * (FL // 128) + i * rows_per + k, 1), :] = down[
                    :, k * 128 : (k + 1) * 128
                ]

    diag = eye(DL, DL)
    rsend[...] = jnp.zeros_like(rsend)
    for m in range(3):
        sums = jnp.sum(racc[m], axis=1, keepdims=True)
        rsend[m : m + 1, :] = jnp.sum(jnp.where(diag, sums, 0.0), axis=0, keepdims=True)
    enter(me, c)
    c_copies = exchange(
        "row", me, NR,
        lambda peer: csend.at[pl.ds(pl.multiple_of(peer * 8, 8), 8), :],
        lambda d: cin.at[d - 1], c_ss, c_rs,
    )
    r_copies = exchange(
        "col", c, NC, lambda peer: rsend, lambda d: rin.at[d - 1], r_ss, r_rs
    )
    mine = pl.ds(pl.multiple_of(me * 8, 8), 8)
    for copy in c_copies:
        copy.wait_recv()
    cfull[mine, :] = csend[mine, :] + jnp.sum(cin[...], axis=0)
    a_copies = exchange(
        "row", me, NR, lambda peer: cfull.at[mine, :], lambda d: cfull.at[mine, :], a_ss, a_rs
    )
    for copy in r_copies:
        copy.wait_recv()
    row_sum = rsend[...] + jnp.sum(rin[...], axis=0)
    row_new = 0.8 * row_old[...] + 0.2 * (row_sum[0:3] / FF + 1e-30)
    row_out[...] = row_new
    for copy in a_copies:
        copy.wait_recv()
    for m in range(3):
        for k in range(FL // 128):
            at = m * (FL // 128) + k
            cflat[m : m + 1, k * 128 : (k + 1) * 128] = cfull[at : at + 1, :]
    col_new = 0.8 * col_old[...] + 0.2 * (cflat[...] / D + 1e-30)
    col_out[...] = col_new
    cinv[...] = 1.0 / col_new
    row_inv = 1.0 / row_new
    racc[...] = jnp.zeros_like(racc)
    for m in range(3):
        @pl.loop(0, tiles)
        def _(i):
            lanes = pl.ds(pl.multiple_of(i * TILE, 128), TILE)
            grad = values[m, :, lanes]
            square = grad * grad * cinv[m : m + 1, lanes]
            folded = square[:, 0:128]
            for k in range(1, rows_per):
                folded = folded + square[:, k * 128 : (k + 1) * 128]
            racc[m] += folded
        column = jnp.sum(jnp.where(diag, row_inv[m : m + 1], 0.0), axis=1, keepdims=True)
        qsend[m : m + 1, :] = jnp.sum(racc[m] * column, axis=0, keepdims=True)
    qsend[3:8, :] = loss_in[3:8, :]
    q_copies = exchange(
        "row", me, NR, lambda peer: qsend, lambda d: qin.at[d - 1], q_ss, q_rs
    )
    for copy in q_copies:
        copy.wait_recv()
    qmid[...] = qsend[...] + jnp.sum(qin[...], axis=0)
    l_copies = exchange(
        "col", c, NC, lambda peer: qmid, lambda d: qmid_in.at[d - 1], l_ss, l_rs
    )
    for copy in l_copies:
        copy.wait_recv()
    total_out[...] = qmid[...] + jnp.sum(qmid_in[...], axis=0)
    for copy in c_copies + r_copies + a_copies + q_copies + l_copies:
        copy.wait_send()


def stats(normed, dy, hidden, grads, row_old, col_old, loss):
    sem = pltpu.SemaphoreType.DMA
    return pl.pallas_call(
        stats_kernel,
        out_shape=(
            jax.ShapeDtypeStruct((3, DL), F32),
            jax.ShapeDtypeStruct((3, FL), F32),
            jax.ShapeDtypeStruct((8, 128), F32),
        ),
        in_specs=[whole()] * 7,
        out_specs=(whole(),) * 3,
        scratch_shapes=[
            pltpu.VMEM((2, DL, TOKENS), BF16),
            pltpu.VMEM((3, DL, FL), F32),
            pltpu.VMEM((3, DL, 128), F32),
            pltpu.VMEM((128, 128), F32),
            pltpu.VMEM((NR - 1, 8, 128), F32),
            pltpu.VMEM((128, 128), F32),
            pltpu.VMEM((8, DL), F32),
            pltpu.VMEM((NC - 1, 8, DL), F32),
            pltpu.VMEM((3, FL), F32),
            pltpu.VMEM((3, FL), F32),
            pltpu.VMEM((8, 128), F32),
            pltpu.VMEM((NR - 1, 8, 128), F32),
            pltpu.VMEM((8, 128), F32),
            pltpu.VMEM((NC - 1, 8, 128), F32),
            sem((NR - 1,)), sem((NR - 1,)), sem((NR - 1,)), sem((NR - 1,)),
            sem((NC - 1,)), sem((NC - 1,)), sem((NR - 1,)), sem((NR - 1,)),
            sem((NC - 1,)), sem((NC - 1,)),
        ],
        compiler_params=pltpu.CompilerParams(
            collective_id=1, has_side_effects=True, vmem_limit_bytes=VMEM_LIMIT
        ),
        name="stats",
    )(normed, dy, hidden, grads, row_old, col_old, loss)


def update_kernel(normed, dy, hidden, gate_in, up_in, row_new, col_new, total, out0, out1, out2, left, scale):
    @pl.when(pl.program_id(0) == 0)
    def _():
        left[0] = normed[...].astype(F32).T.astype(BF16)
        left[1] = dy[...].astype(F32).T.astype(BF16)
        diag = eye(DL, DL)
        for m in range(3):
            mean = jnp.sum(total[m : m + 1, :], axis=1, keepdims=True) / (float(D) * FF)
            clip = 1.0 / jnp.maximum(1.0, jnp.sqrt(mean))
            column = jnp.sum(
                jnp.where(diag, row_new[m : m + 1, :], 0.0), axis=1, keepdims=True
            )
            scale[m] = jnp.broadcast_to(clip / jnp.sqrt(column), (DL, 128))

    for m, (lhs, rhs, out) in enumerate(
        ((left[0], gate_in, out0), (left[0], up_in, out1), (left[1], hidden, out2))
    ):
        grad = jnp.dot(lhs, rhs[...], preferred_element_type=F32)
        lane = 1.0 / jnp.sqrt(col_new[m : m + 1, :])
        for k in range(TILE // 128):
            at = slice(k * 128, (k + 1) * 128)
            out[:, at] = (grad[:, at] * scale[m] * lane[:, at]).astype(BF16)


def update(normed, dy, hidden, grads, row_new, col_new, total):
    full = lambda shape: pl.BlockSpec(shape, lambda i: (0, 0))
    tile = pl.BlockSpec((DL, TILE), lambda i: (0, i))
    half = FH // TILE
    return pl.pallas_call(
        update_kernel,
        grid=(FL // TILE,),
        out_shape=(jax.ShapeDtypeStruct((DL, FL), BF16),) * 3,
        in_specs=[
            full((TOKENS, DL)),
            full((TOKENS, DL)),
            pl.BlockSpec((TOKENS, TILE), lambda i: (0, i)),
            pl.BlockSpec((TOKENS, TILE), lambda i: (0, i + lax.div(i, half) * half)),
            pl.BlockSpec((TOKENS, TILE), lambda i: (0, i + half + lax.div(i, half) * half)),
            full((3, DL)),
            pl.BlockSpec((3, TILE), lambda i: (0, i)),
            full((8, 128)),
        ],
        out_specs=(tile,) * 3,
        scratch_shapes=[pltpu.VMEM((2, DL, TOKENS), BF16), pltpu.VMEM((3, DL, 128), F32)],
        compiler_params=pltpu.CompilerParams(dimension_semantics=("arbitrary",)),
        name="update",
    )(normed, dy, hidden, grads, grads, row_new, col_new, total)


def shards(teacher_rows, projection, student_in, norm_gain, w_gate, w_up, w_down, row_old, col_old):
    normed, dy, hidden, grads, loss = step(
        teacher_rows, projection, student_in, norm_gain[None, :], w_gate, w_up, w_down
    )
    row_new, col_new, total = stats(normed, dy, hidden, grads, row_old, col_old, loss)
    out = update(normed, dy, hidden, grads, row_new, col_new, total)
    return (*out, row_new, col_new, 0.5 * total[3, 0] / TOKENS)


def solution(mesh):
    placed = (
        P("col", "row"),
        P("row", None),
        P("col", "row"),
        P("row"),
        P("row", "col"),
        P("row", "col"),
        P("row", "col"),
        P(None, "row"),
        P(None, "col"),
    )
    return jax.shard_map(
        shards,
        mesh=mesh,
        in_specs=placed,
        out_specs=(
            P("row", "col"),
            P("row", "col"),
            P("row", "col"),
            P(None, "row"),
            P(None, "col"),
            P(),
        ),
        check_vma=False,
    )
```

```python
import math

import jax
import jax.numpy as jnp
from jax import lax
from jax.experimental import pallas as pl
from jax.experimental.pallas import tpu as pltpu
from jax.sharding import PartitionSpec as P

D = 4608
FF = 36864
TOKENS = 256
NR = 16
NC = 8
DL = D // NR
FL = FF // NC
TL = TOKENS // NC
TILE = 768
F32 = jnp.float32
BF16 = jnp.bfloat16
VMEM_LIMIT = 67_000_000


def gelu_pair(values):
    root_coef = math.sqrt(2.0 / math.pi)
    tangent = jnp.tanh(root_coef * (values + 0.044715 * values * values * values))
    gelu_val = 0.5 * values * (1.0 + tangent)
    gelu_slope = 0.5 * (1.0 + tangent) + 0.5 * values * (1.0 - tangent * tangent) * root_coef * (
        1.0 + 3.0 * 0.044715 * values * values
    )
    return (gelu_val, gelu_slope)


def remote(src, dst, send_sem, recv_sem, axis, index):
    return pltpu.make_async_remote_copy(
        src_ref=src,
        dst_ref=dst,
        send_sem=send_sem,
        recv_sem=recv_sem,
        device_id={axis: index},
        device_id_type=pl.DeviceIdType.MESH,
    )


def greet(me, c):
    barrier = pltpu.get_barrier_semaphore()
    for d in range(1, NR):
        pl.semaphore_signal(
            barrier, inc=1, device_id={"row": lax.rem(me + d, NR)},
            device_id_type=pl.DeviceIdType.MESH,
        )
    for d in range(1, NC):
        pl.semaphore_signal(
            barrier, inc=1, device_id={"col": lax.rem(c + d, NC)},
            device_id_type=pl.DeviceIdType.MESH,
        )


def met():
    pl.semaphore_wait(pltpu.get_barrier_semaphore(), NR + NC - 2)


def exchange(axis, me, n, source, slots, send_sem, recv_sem):
    copies = []
    for d in range(1, n):
        peer = lax.rem(me + d, n)
        copy = remote(
            source(peer), slots(d), send_sem.at[d - 1], recv_sem.at[d - 1], axis, peer
        )
        copy.start()
        copies.append(copy)
    return copies


def finish(copies):
    for copy in copies:
        copy.wait_recv()
    for copy in copies:
        copy.wait_send()


class Scatter:
    def __init__(self, buf, wide, rows, lo, wide_lo, width, p, plus, minus, recv, acc, ss, rs):
        self.buf, self.wide, self.rows = buf, wide, rows
        self.lo, self.wide_lo, self.half = lo, wide_lo, width // 2
        self.p, self.plus, self.minus = p, plus, minus
        self.recv, self.acc, self.ss, self.rs = recv, acc, ss, rs

    def part(self, k, which):
        at = pl.multiple_of(lax.rem(self.p + k, 4) * self.rows, 16)
        return self.buf.at[pl.ds(at, self.rows), pl.ds(self.lo + which * self.half, self.half)]

    def own(self, k, which):
        at = pl.multiple_of(lax.rem(self.p + k, 4) * self.rows, 16)
        return self.wide[pl.ds(at, self.rows), pl.ds(self.wide_lo + which * self.half, self.half)]

    def send(self, src, slot, to):
        copy = remote(
            src, self.recv.at[slot], self.ss.at[slot], self.rs.at[slot], "row", to
        )
        copy.start()
        return copy

    def start(self):
        self.copies = [
            self.send(self.part(2, 0), 0, self.plus),
            self.send(self.part(2, 1), 1, self.minus),
            self.send(self.part(1, 1), 2, self.plus),
            self.send(self.part(3, 0), 3, self.minus),
        ]

    def relay(self):
        self.copies[0].wait_recv()
        self.acc[0] = (self.own(1, 0) + self.recv[0].astype(F32)).astype(BF16)
        self.copies.append(self.send(self.acc.at[0], 4, self.plus))
        self.copies[1].wait_recv()
        self.acc[1] = (self.own(3, 1) + self.recv[1].astype(F32)).astype(BF16)
        self.copies.append(self.send(self.acc.at[1], 5, self.minus))

    def result(self):
        for at in (3, 2, 4, 5):
            self.copies[at].wait_recv()
        first = self.own(0, 0) + self.recv[3].astype(F32) + self.recv[4].astype(F32)
        second = self.own(0, 1) + self.recv[2].astype(F32) + self.recv[5].astype(F32)
        return (first, second)

    def drain(self):
        for copy in self.copies:
            copy.wait_send()


class Gather:
    def __init__(self, buf, base, rows, lo, width, p, plus, minus, ss, rs):
        self.buf, self.base, self.rows, self.lo, self.width = buf, base, rows, lo, width
        self.p, self.plus, self.minus, self.ss, self.rs = p, plus, minus, ss, rs

    def part(self, k, lo, width):
        at = pl.multiple_of(self.base + lax.rem(self.p + k, 4) * self.rows, 16)
        return self.buf.at[pl.ds(at, self.rows), pl.ds(self.lo + lo, width)]

    def send(self, ref, slot, to):
        copy = remote(ref, ref, self.ss.at[slot], self.rs.at[slot], "row", to)
        copy.start()
        return copy

    def start(self):
        self.copies = [
            self.send(self.part(0, 0, self.width), 0, self.plus),
            self.send(self.part(0, 0, self.width), 1, self.minus),
        ]

    def relay(self):
        half = self.width // 2
        self.copies[0].wait_recv()
        self.copies.append(self.send(self.part(3, 0, half), 2, self.plus))
        self.copies[1].wait_recv()
        self.copies.append(self.send(self.part(1, half, half), 3, self.minus))

    def done(self):
        self.copies[2].wait_recv()
        self.copies[3].wait_recv()

    def drain(self):
        for copy in self.copies:
            copy.wait_send()


def eye(rows, lanes):
    return lax.broadcasted_iota(jnp.int32, (rows, lanes), 0) == lax.broadcasted_iota(
        jnp.int32, (rows, lanes), 1
    )


def step_kernel(
    teacher, projection, student, gain, w_gate, w_up, w_down, row_old, col_old,
    normed_out, dy_out, hidden_out, grads_out, row_out, col_out, total_out,
    proj_v, wg_v, wu_v, wd_v, sq, sq_in, tpart, tpart_in, normed, part, mid, mid32, recv1, acc1,
    recv2, acc2, hidden, act_v, ups_v, down_acc, down_part, down_in, dy, gpart, gmid, gmid32,
    grecv1, gacc1, grecv2, gacc2, grads, big,
    left, racc, csend, cin, cfull, rsend, rin, cflat, cinv, qsend, qin, qmid, qmid_in,
    load_sem, out_sem, sq_ss, sq_rs, t_ss, t_rs, n_ss, n_rs, d_ss, d_rs, y_ss, y_rs,
    s_ss, s_rs, g_ss, g_rs,
    c_ss, c_rs, a_ss, a_rs, r_ss, r_rs, q_ss, q_rs, l_ss, l_rs,
):
    me = lax.axis_index("row")
    c = lax.axis_index("col")
    x, z = lax.div(me, 4), lax.rem(me, 4)
    greet(me, c)
    loads = [
        pltpu.make_async_copy(src, dst, load_sem.at[i])
        for i, (src, dst) in enumerate(
            ((projection, proj_v), (w_gate, wg_v), (w_up, wu_v), (w_down, wd_v))
        )
    ]
    for load in loads:
        load.start()
    own = pl.ds(pl.multiple_of(c * TL, TL), TL)
    inputs = student[...].astype(F32)
    diag = eye(TL, 128)
    sums = jnp.sum(inputs * inputs, axis=1, keepdims=True)
    sq[...] = jnp.broadcast_to(
        jnp.sum(jnp.where(diag, sums, 0.0), axis=0, keepdims=True), (8, 128)
    )
    met()
    sq_copies = exchange(
        "row", me, NR, lambda peer: sq, lambda d: sq_in.at[d - 1], sq_ss, sq_rs
    )
    loads[0].wait()
    for i in range(4):
        product = jnp.dot(
            teacher[...], proj_v[:, i * 4 * DL : (i + 1) * 4 * DL], preferred_element_type=F32
        )
        for j in range(4):
            tpart[i * 4 + j] = product[:, j * DL : (j + 1) * DL].astype(BF16)
    t_copies = exchange(
        "row", me, NR, lambda peer: tpart.at[peer], lambda d: tpart_in.at[d - 1], t_ss, t_rs
    )
    for copy in sq_copies:
        copy.wait_recv()
    total = sq[0:1] + jnp.sum(sq_in[:, 0, :], axis=0, keepdims=True)
    mean_sq = jnp.sum(jnp.where(diag, total, 0.0), axis=1, keepdims=True) / D
    inv_rms = 1.0 / jnp.sqrt(mean_sq + 1e-06)
    normed[own, :] = (inputs * inv_rms * gain[...].astype(F32)).astype(BF16)
    n_copies = exchange(
        "col", c, NC, lambda peer: normed.at[own, :], lambda d: normed.at[own, :], n_ss, n_rs
    )
    for copy in n_copies:
        copy.wait_recv()
    for load in loads[1:]:
        load.wait()

    xp, xm = lax.rem(x + 1, 4) * 4 + z, lax.rem(x + 3, 4) * 4 + z
    zp, zm = x * 4 + lax.rem(z + 1, 4), x * 4 + lax.rem(z + 3, 4)
    first = ((x, xp, xm), (z, zp, zm))
    second = ((z, zp, zm), (x, xp, xm))
    drains = []

    def owner(s):
        base = pl.multiple_of(first[s][0] * 64, 64)
        return base, pl.ds(pl.multiple_of(base + second[s][0] * 16, 16), 16)

    def sub(lo, i):
        return pl.ds(pl.multiple_of(lo + i * 256, 128), 256)

    def run(stages):
        for t in range(len(stages) + 2):
            order = [j for j in range(3) if t == j] + [
                j for j in range(3) if 0 < t - j < len(stages)
            ]
            for j in order:
                for s in range(2):
                    stages[t - j](s, j)

    sc1, sc2, ga1, ga2 = {}, {}, {}, {}

    def f_start(s, j):
        k = 3 * s + j

        @pl.loop(0, 3)
        def _(i):
            rows = normed[...]
            for weights, off in ((wg_v, 0), (wu_v, TILE)):
                value = jnp.dot(rows, weights[:, sub(k * TILE, i)], preferred_element_type=F32)
                big[s * TOKENS : (s + 1) * TOKENS, sub(j * 2 * TILE + off, i)] = value
                part[:, sub(k * 2 * TILE + off, i)] = value.astype(BF16)

        sc1[k] = Scatter(
            part, big.at[s * TOKENS : (s + 1) * TOKENS], 64, k * 2 * TILE, j * 2 * TILE, 2 * TILE,
            *first[s], recv1.at[k], acc1.at[k], s_ss.at[k], s_rs.at[k],
        )
        sc1[k].start()
        drains.append(sc1[k])

    def f_relay1(s, j):
        sc1[3 * s + j].relay()

    def f_second(s, j):
        k = 3 * s + j
        for h, value in enumerate(sc1[k].result()):
            at = slice(h * TILE, (h + 1) * TILE)
            mid32[k, :, at] = value
            mid[k, :, at] = value.astype(BF16)
        sc2[k] = Scatter(
            mid.at[k], mid32.at[k], 16, 0, 0, 2 * TILE, *second[s], recv2.at[k], acc2.at[k],
            s_ss.at[6 + k], s_rs.at[6 + k],
        )
        sc2[k].start()
        drains.append(sc2[k])

    def f_relay2(s, j):
        sc2[3 * s + j].relay()

    def f_hidden(s, j):
        k = 3 * s + j
        gate, up = sc2[k].result()
        act, slope = gelu_pair(gate)
        act_v[k] = act
        ups_v[k] = up * slope
        base, rows = owner(s)
        hidden[rows, k * TILE : (k + 1) * TILE] = (act * up).astype(BF16)
        ga1[k] = Gather(hidden, base, 16, k * TILE, TILE, *second[s], g_ss.at[k], g_rs.at[k])
        ga1[k].start()
        drains.append(ga1[k])

    def f_relay3(s, j):
        ga1[3 * s + j].relay()

    def f_gather(s, j):
        k = 3 * s + j
        ga1[k].done()
        ga2[k] = Gather(
            hidden, 0, 64, k * TILE, TILE, *first[s], g_ss.at[6 + k], g_rs.at[6 + k]
        )
        ga2[k].start()
        drains.append(ga2[k])

    def f_relay4(s, j):
        ga2[3 * s + j].relay()

    down_acc[...] = jnp.zeros_like(down_acc)

    def f_down(s, j):
        k = 3 * s + j
        ga2[k].done()

        @pl.loop(0, 3)
        def _(i):
            lanes = sub(k * TILE, i)
            down_acc[...] += lax.dot_general(
                hidden[:, lanes], wd_v[:, lanes], (((1,), (1,)), ((), ())),
                preferred_element_type=F32,
            )

    run((f_start, f_relay1, f_second, f_relay2, f_hidden, f_relay3, f_gather, f_relay4, f_down))

    down_part[...] = down_acc[...].astype(BF16)
    d_copies = exchange(
        "col", c, NC,
        lambda peer: down_part.at[pl.ds(pl.multiple_of(peer * TL, TL), TL), :],
        lambda d: down_in.at[d - 1], d_ss, d_rs,
    )
    hidden_copy = pltpu.make_async_copy(hidden, hidden_out, out_sem.at[0])
    hidden_copy.start()
    normed_copy = pltpu.make_async_copy(normed, normed_out, out_sem.at[1])
    normed_copy.start()
    finish(t_copies)
    target = tpart[me].astype(F32)
    for d in range(NR - 1):
        target = target + tpart_in[d].astype(F32)
    rest = inputs - target.astype(BF16).astype(F32)
    for copy in d_copies:
        copy.wait_recv()
    down = down_acc[own, :]
    for d in range(NC - 1):
        down = down + down_in[d].astype(F32)
    residue = rest + down
    dy[own, :] = (residue / TOKENS).astype(BF16)
    y_copies = exchange(
        "col", c, NC, lambda peer: dy.at[own, :], lambda d: dy.at[own, :], y_ss, y_rs
    )
    qsend[...] = jnp.zeros_like(qsend) + jnp.sum(residue * residue)
    left[0] = normed[...].astype(F32).T.astype(BF16)
    for copy in y_copies:
        copy.wait_recv()
    dy_copy = pltpu.make_async_copy(dy, dy_out, out_sem.at[2])
    dy_copy.start()

    gs1, gs2, gg1, gg2 = {}, {}, {}, {}
    half = TILE // 2
    csend[...] = jnp.zeros_like(csend)
    racc[...] = jnp.zeros_like(racc)

    def b_start(s, j):
        k = 3 * s + j

        @pl.loop(0, 3)
        def _(i):
            lanes = sub(k * TILE, i)
            value = jnp.dot(dy[...], wd_v[:, lanes], preferred_element_type=F32)
            big[0:TOKENS, lanes] = value
            gpart[:, lanes] = value.astype(BF16)

        gs1[k] = Scatter(
            gpart, big.at[0:TOKENS], 64, k * TILE, k * TILE, TILE, *first[s],
            grecv1.at[k], gacc1.at[k], s_ss.at[12 + k], s_rs.at[12 + k],
        )
        gs1[k].start()
        drains.append(gs1[k])

    def b_relay1(s, j):
        gs1[3 * s + j].relay()

    def b_second(s, j):
        k = 3 * s + j
        for h, value in enumerate(gs1[k].result()):
            at = slice(h * half, (h + 1) * half)
            gmid32[k, :, at] = value
            gmid[k, :, at] = value.astype(BF16)
        gs2[k] = Scatter(
            gmid.at[k], gmid32.at[k], 16, 0, 0, TILE, *second[s], grecv2.at[k], gacc2.at[k],
            s_ss.at[18 + k], s_rs.at[18 + k],
        )
        gs2[k].start()
        drains.append(gs2[k])

    def b_relay2(s, j):
        gs2[3 * s + j].relay()

    def b_inputs(s, j):
        k = 3 * s + j
        base, rows = owner(s)
        for h, value in enumerate(gs2[k].result()):
            at = slice(h * half, (h + 1) * half)
            lo = 2 * k * TILE + h * half
            grads[rows, lo : lo + half] = (value * ups_v[k, :, at]).astype(BF16)
            lo = lo + TILE
            grads[rows, lo : lo + half] = (value * act_v[k, :, at]).astype(BF16)
        gg1[k] = Gather(
            grads, base, 16, 2 * k * TILE, 2 * TILE, *second[s], g_ss.at[12 + k], g_rs.at[12 + k]
        )
        gg1[k].start()
        drains.append(gg1[k])

    def b_relay3(s, j):
        gg1[3 * s + j].relay()

    def b_gather(s, j):
        k = 3 * s + j
        gg1[k].done()
        gg2[k] = Gather(
            grads, 0, 64, 2 * k * TILE, 2 * TILE, *first[s], g_ss.at[18 + k], g_rs.at[18 + k]
        )
        gg2[k].start()
        drains.append(gg2[k])

    def b_relay4(s, j):
        gg2[3 * s + j].relay()

    def sums_of(m, k, rhs, lo):
        @pl.loop(0, 3)
        def _(i):
            grad = jnp.dot(left[m // 2], rhs[:, sub(lo, i)], preferred_element_type=F32)
            big[m * DL : (m + 1) * DL, sub(k * TILE, i)] = grad
            square = grad * grad
            racc[m] += square[:, 0:128] + square[:, 128:256]
            column = jnp.sum(square, axis=0, keepdims=True)
            for n in range(2):
                csend[pl.ds(m * (FL // 128) + k * 6 + i * 2 + n, 1), :] = column[
                    :, n * 128 : (n + 1) * 128
                ]

    def b_sums(s, j):
        k = 3 * s + j
        gg2[k].done()
        sums_of(0, k, grads, 2 * k * TILE)
        sums_of(1, k, grads, (2 * k + 1) * TILE)

    def b_relay1_and_down(s, j):
        if s == 0 and j == 0:
            left[1] = dy[...].astype(F32).T.astype(BF16)
        b_relay1(s, j)
        sums_of(2, 3 * s + j, hidden, (3 * s + j) * TILE)

    run(
        (
            b_start, b_relay1_and_down, b_second, b_relay2, b_inputs, b_relay3, b_gather,
            b_relay4, b_sums,
        )
    )
    grads_copy = pltpu.make_async_copy(grads, grads_out, out_sem.at[3])
    grads_copy.start()

    c_copies = exchange(
        "row", me, NR,
        lambda peer: csend.at[pl.ds(pl.multiple_of(peer * 8, 8), 8), :],
        lambda d: cin.at[d - 1], c_ss, c_rs,
    )
    wide = eye(DL, DL)
    rsend[...] = jnp.zeros_like(rsend)
    for m in range(3):
        sums = jnp.sum(racc[m], axis=1, keepdims=True)
        rsend[m : m + 1, :] = jnp.sum(jnp.where(wide, sums, 0.0), axis=0, keepdims=True)
    r_copies = exchange(
        "col", c, NC, lambda peer: rsend, lambda d: rin.at[d - 1], r_ss, r_rs
    )
    mine = pl.ds(pl.multiple_of(me * 8, 8), 8)
    for copy in c_copies:
        copy.wait_recv()
    cfull[mine, :] = csend[mine, :] + jnp.sum(cin[...], axis=0)
    a_copies = exchange(
        "row", me, NR, lambda peer: cfull.at[mine, :], lambda d: cfull.at[mine, :], a_ss, a_rs
    )
    for copy in r_copies:
        copy.wait_recv()
    row_sum = rsend[...] + jnp.sum(rin[...], axis=0)
    row_new = 0.8 * row_old[...] + 0.2 * (row_sum[0:3] / FF + 1e-30)
    row_out[...] = row_new
    row_inv = 1.0 / row_new
    columns = [
        jnp.sum(jnp.where(wide, row_inv[m : m + 1], 0.0), axis=1, keepdims=True) for m in range(3)
    ]
    for copy in a_copies:
        copy.wait_recv()
    for m in range(3):
        for k in range(FL // 128):
            at = m * (FL // 128) + k
            cflat[m : m + 1, k * 128 : (k + 1) * 128] = cfull[at : at + 1, :]
    col_new = 0.8 * col_old[...] + 0.2 * (cflat[...] / D + 1e-30)
    col_out[...] = col_new
    cinv[...] = 1.0 / col_new
    racc[...] = jnp.zeros_like(racc)
    for m in range(3):
        @pl.loop(0, FL // 256)
        def _(i):
            lanes = sub(0, i)
            grad = big[m * DL : (m + 1) * DL, lanes]
            square = grad * grad * cinv[m : m + 1, lanes]
            racc[m] += square[:, 0:128] + square[:, 128:256]
        qsend[m : m + 1, :] = jnp.sum(racc[m] * columns[m], axis=0, keepdims=True)
    q_copies = exchange(
        "row", me, NR, lambda peer: qsend, lambda d: qin.at[d - 1], q_ss, q_rs
    )
    for copy in q_copies:
        copy.wait_recv()
    qmid[...] = qsend[...] + jnp.sum(qin[...], axis=0)
    l_copies = exchange(
        "col", c, NC, lambda peer: qmid, lambda d: qmid_in.at[d - 1], l_ss, l_rs
    )
    for copy in l_copies:
        copy.wait_recv()
    total_out[...] = qmid[...] + jnp.sum(qmid_in[...], axis=0)
    for copy in sq_copies + n_copies + d_copies + y_copies:
        copy.wait_send()
    for copy in c_copies + r_copies + a_copies + q_copies + l_copies:
        copy.wait_send()
    for one in drains:
        one.drain()
    for copy in (hidden_copy, normed_copy, dy_copy, grads_copy):
        copy.wait()


def whole(space=pltpu.VMEM):
    return pl.BlockSpec(memory_space=space)


def step(teacher, projection, student, gain, w_gate, w_up, w_down, row_old, col_old):
    sem = pltpu.SemaphoreType.DMA
    half = TILE // 2
    return pl.pallas_call(
        step_kernel,
        out_shape=(
            jax.ShapeDtypeStruct((TOKENS, DL), BF16),
            jax.ShapeDtypeStruct((TOKENS, DL), BF16),
            jax.ShapeDtypeStruct((TOKENS, FL), BF16),
            jax.ShapeDtypeStruct((TOKENS, 2 * FL), BF16),
            jax.ShapeDtypeStruct((3, DL), F32),
            jax.ShapeDtypeStruct((3, FL), F32),
            jax.ShapeDtypeStruct((8, 128), F32),
        ),
        in_specs=[
            whole(), whole(pl.ANY), whole(), whole(), whole(pl.ANY), whole(pl.ANY), whole(pl.ANY),
            whole(), whole(),
        ],
        out_specs=(whole(pl.ANY),) * 4 + (whole(),) * 3,
        scratch_shapes=[
            pltpu.VMEM(projection.shape, BF16),
            pltpu.VMEM((DL, FL), BF16),
            pltpu.VMEM((DL, FL), BF16),
            pltpu.VMEM((DL, FL), BF16),
            pltpu.VMEM((8, 128), F32),
            pltpu.VMEM((NR - 1, 8, 128), F32),
            pltpu.VMEM((NR, TL, DL), BF16),
            pltpu.VMEM((NR - 1, TL, DL), BF16),
            pltpu.VMEM((TOKENS, DL), BF16),
            pltpu.VMEM((TOKENS, 2 * FL), BF16),
            pltpu.VMEM((6, 64, 2 * TILE), BF16),
            pltpu.VMEM((6, 64, 2 * TILE), F32),
            pltpu.VMEM((6, 6, 64, TILE), BF16),
            pltpu.VMEM((6, 2, 64, TILE), BF16),
            pltpu.VMEM((6, 6, 16, TILE), BF16),
            pltpu.VMEM((6, 2, 16, TILE), BF16),
            pltpu.VMEM((TOKENS, FL), BF16),
            pltpu.VMEM((6, 16, TILE), F32),
            pltpu.VMEM((6, 16, TILE), F32),
            pltpu.VMEM((TOKENS, DL), F32),
            pltpu.VMEM((TOKENS, DL), BF16),
            pltpu.VMEM((NC - 1, TL, DL), BF16),
            pltpu.VMEM((TOKENS, DL), BF16),
            pltpu.VMEM((TOKENS, FL), BF16),
            pltpu.VMEM((6, 64, TILE), BF16),
            pltpu.VMEM((6, 64, TILE), F32),
            pltpu.VMEM((6, 6, 64, half), BF16),
            pltpu.VMEM((6, 2, 64, half), BF16),
            pltpu.VMEM((6, 6, 16, half), BF16),
            pltpu.VMEM((6, 2, 16, half), BF16),
            pltpu.VMEM((TOKENS, 2 * FL), BF16),
            pltpu.VMEM((3 * DL, FL), F32),
            pltpu.VMEM((2, DL, TOKENS), BF16),
            pltpu.VMEM((3, DL, 128), F32),
            pltpu.VMEM((128, 128), F32),
            pltpu.VMEM((NR - 1, 8, 128), F32),
            pltpu.VMEM((128, 128), F32),
            pltpu.VMEM((8, DL), F32),
            pltpu.VMEM((NC - 1, 8, DL), F32),
            pltpu.VMEM((3, FL), F32),
            pltpu.VMEM((3, FL), F32),
            pltpu.VMEM((8, 128), F32),
            pltpu.VMEM((NR - 1, 8, 128), F32),
            pltpu.VMEM((8, 128), F32),
            pltpu.VMEM((NC - 1, 8, 128), F32),
            sem((4,)), sem((4,)),
            sem((NR - 1,)), sem((NR - 1,)), sem((NR - 1,)), sem((NR - 1,)),
            sem((NC - 1,)), sem((NC - 1,)), sem((NC - 1,)), sem((NC - 1,)),
            sem((NC - 1,)), sem((NC - 1,)),
            sem((24, 6)), sem((24, 6)), sem((24, 4)), sem((24, 4)),
            sem((NR - 1,)), sem((NR - 1,)), sem((NR - 1,)), sem((NR - 1,)),
            sem((NC - 1,)), sem((NC - 1,)), sem((NR - 1,)), sem((NR - 1,)),
            sem((NC - 1,)), sem((NC - 1,)),
        ],
        compiler_params=pltpu.CompilerParams(
            collective_id=0, has_side_effects=True, vmem_limit_bytes=VMEM_LIMIT
        ),
        name="step",
    )(teacher, projection, student, gain, w_gate, w_up, w_down, row_old, col_old)


def update_kernel(normed, dy, hidden, gate_in, up_in, row_new, col_new, total, out0, out1, out2, left, scale):
    @pl.when(pl.program_id(0) == 0)
    def _():
        left[0] = normed[...].astype(F32).T.astype(BF16)
        left[1] = dy[...].astype(F32).T.astype(BF16)
        diag = eye(DL, DL)
        for m in range(3):
            mean = jnp.sum(total[m : m + 1, :], axis=1, keepdims=True) / (float(D) * FF)
            clip = 1.0 / jnp.maximum(1.0, jnp.sqrt(mean))
            column = jnp.sum(
                jnp.where(diag, row_new[m : m + 1, :], 0.0), axis=1, keepdims=True
            )
            scale[m] = jnp.broadcast_to(clip / jnp.sqrt(column), (DL, 128))

    for m, (lhs, rhs, out) in enumerate(
        ((left[0], gate_in, out0), (left[0], up_in, out1), (left[1], hidden, out2))
    ):
        grad = jnp.dot(lhs, rhs[...], preferred_element_type=F32)
        lane = 1.0 / jnp.sqrt(col_new[m : m + 1, :])
        for k in range(TILE // 128):
            at = slice(k * 128, (k + 1) * 128)
            out[:, at] = (grad[:, at] * scale[m] * lane[:, at]).astype(BF16)


def update(normed, dy, hidden, grads, row_new, col_new, total):
    full = lambda shape: pl.BlockSpec(shape, lambda i: (0, 0))
    tile = pl.BlockSpec((DL, TILE), lambda i: (0, i))
    return pl.pallas_call(
        update_kernel,
        grid=(FL // TILE,),
        out_shape=(jax.ShapeDtypeStruct((DL, FL), BF16),) * 3,
        in_specs=[
            full((TOKENS, DL)),
            full((TOKENS, DL)),
            pl.BlockSpec((TOKENS, TILE), lambda i: (0, i)),
            pl.BlockSpec((TOKENS, TILE), lambda i: (0, 2 * i)),
            pl.BlockSpec((TOKENS, TILE), lambda i: (0, 2 * i + 1)),
            full((3, DL)),
            pl.BlockSpec((3, TILE), lambda i: (0, i)),
            full((8, 128)),
        ],
        out_specs=(tile,) * 3,
        scratch_shapes=[pltpu.VMEM((2, DL, TOKENS), BF16), pltpu.VMEM((3, DL, 128), F32)],
        compiler_params=pltpu.CompilerParams(dimension_semantics=("arbitrary",)),
        name="update",
    )(normed, dy, hidden, grads, grads, row_new, col_new, total)


def shards(teacher_rows, projection, student_in, norm_gain, w_gate, w_up, w_down, row_old, col_old):
    normed, dy, hidden, grads, row_new, col_new, total = step(
        teacher_rows, projection, student_in, norm_gain[None, :], w_gate, w_up, w_down,
        row_old, col_old,
    )
    out = update(normed, dy, hidden, grads, row_new, col_new, total)
    return (*out, row_new, col_new, 0.5 * total[3, 0] / TOKENS)


def solution(mesh):
    placed = (
        P("col", "row"),
        P("row", None),
        P("col", "row"),
        P("row"),
        P("row", "col"),
        P("row", "col"),
        P("row", "col"),
        P(None, "row"),
        P(None, "col"),
    )
    return jax.shard_map(
        shards,
        mesh=mesh,
        in_specs=placed,
        out_specs=(
            P("row", "col"),
            P("row", "col"),
            P("row", "col"),
            P(None, "row"),
            P(None, "col"),
            P(),
        ),
        check_vma=False,
    )
```

```python
import math

import jax
import jax.numpy as jnp
from jax import lax
from jax.experimental import pallas as pl
from jax.experimental.pallas import tpu as pltpu
from jax.sharding import PartitionSpec as P

D = 4608
FF = 36864
TOKENS = 256
NR = 16
NC = 8
DL = D // NR
FL = FF // NC
TL = TOKENS // NC
TILE = 768
F32 = jnp.float32
BF16 = jnp.bfloat16
VMEM_LIMIT = 67_000_000


def gelu_pair(values):
    root_coef = math.sqrt(2.0 / math.pi)
    tangent = jnp.tanh(root_coef * (values + 0.044715 * values * values * values))
    gelu_val = 0.5 * values * (1.0 + tangent)
    gelu_slope = 0.5 * (1.0 + tangent) + 0.5 * values * (1.0 - tangent * tangent) * root_coef * (
        1.0 + 3.0 * 0.044715 * values * values
    )
    return (gelu_val, gelu_slope)


def remote(src, dst, send_sem, recv_sem, axis, index):
    return pltpu.make_async_remote_copy(
        src_ref=src,
        dst_ref=dst,
        send_sem=send_sem,
        recv_sem=recv_sem,
        device_id={axis: index},
        device_id_type=pl.DeviceIdType.MESH,
    )


def greet(me, c):
    barrier = pltpu.get_barrier_semaphore()
    for d in range(1, NR):
        pl.semaphore_signal(
            barrier, inc=1, device_id={"row": lax.rem(me + d, NR)},
            device_id_type=pl.DeviceIdType.MESH,
        )
    for d in range(1, NC):
        pl.semaphore_signal(
            barrier, inc=1, device_id={"col": lax.rem(c + d, NC)},
            device_id_type=pl.DeviceIdType.MESH,
        )


def met():
    pl.semaphore_wait(pltpu.get_barrier_semaphore(), NR + NC - 2)


def exchange(axis, me, n, source, slots, send_sem, recv_sem):
    copies = []
    for d in range(1, n):
        peer = lax.rem(me + d, n)
        copy = remote(
            source(peer), slots(d), send_sem.at[d - 1], recv_sem.at[d - 1], axis, peer
        )
        copy.start()
        copies.append(copy)
    return copies


def finish(copies):
    for copy in copies:
        copy.wait_recv()
    for copy in copies:
        copy.wait_send()


class Scatter:
    def __init__(self, buf, wide, rows, lo, wide_lo, width, p, plus, minus, recv, acc, ss, rs):
        self.buf, self.wide, self.rows = buf, wide, rows
        self.lo, self.wide_lo, self.half = lo, wide_lo, width // 2
        self.p, self.plus, self.minus = p, plus, minus
        self.recv, self.acc, self.ss, self.rs = recv, acc, ss, rs

    def part(self, k, which):
        at = pl.multiple_of(lax.rem(self.p + k, 4) * self.rows, 16)
        return self.buf.at[pl.ds(at, self.rows), pl.ds(self.lo + which * self.half, self.half)]

    def own(self, k, which):
        at = pl.multiple_of(lax.rem(self.p + k, 4) * self.rows, 16)
        return self.wide[pl.ds(at, self.rows), pl.ds(self.wide_lo + which * self.half, self.half)]

    def send(self, src, slot, to):
        copy = remote(
            src, self.recv.at[slot], self.ss.at[slot], self.rs.at[slot], "row", to
        )
        copy.start()
        return copy

    def start(self):
        self.copies = [
            self.send(self.part(2, 0), 0, self.plus),
            self.send(self.part(2, 1), 1, self.minus),
            self.send(self.part(1, 1), 2, self.plus),
            self.send(self.part(3, 0), 3, self.minus),
        ]

    def relay(self):
        self.copies[0].wait_recv()
        self.acc[0] = (self.own(1, 0) + self.recv[0].astype(F32)).astype(BF16)
        self.copies.append(self.send(self.acc.at[0], 4, self.plus))
        self.copies[1].wait_recv()
        self.acc[1] = (self.own(3, 1) + self.recv[1].astype(F32)).astype(BF16)
        self.copies.append(self.send(self.acc.at[1], 5, self.minus))

    def result(self):
        for at in (3, 2, 4, 5):
            self.copies[at].wait_recv()
        first = self.own(0, 0) + self.recv[3].astype(F32) + self.recv[4].astype(F32)
        second = self.own(0, 1) + self.recv[2].astype(F32) + self.recv[5].astype(F32)
        return (first, second)

    def drain(self):
        for copy in self.copies:
            copy.wait_send()


class Gather:
    def __init__(self, buf, base, rows, lo, width, p, plus, minus, ss, rs):
        self.buf, self.base, self.rows, self.lo, self.width = buf, base, rows, lo, width
        self.p, self.plus, self.minus, self.ss, self.rs = p, plus, minus, ss, rs

    def part(self, k, lo, width):
        at = pl.multiple_of(self.base + lax.rem(self.p + k, 4) * self.rows, 16)
        return self.buf.at[pl.ds(at, self.rows), pl.ds(self.lo + lo, width)]

    def send(self, ref, slot, to):
        copy = remote(ref, ref, self.ss.at[slot], self.rs.at[slot], "row", to)
        copy.start()
        return copy

    def start(self):
        self.copies = [
            self.send(self.part(0, 0, self.width), 0, self.plus),
            self.send(self.part(0, 0, self.width), 1, self.minus),
        ]

    def relay(self):
        half = self.width // 2
        self.copies[0].wait_recv()
        self.copies.append(self.send(self.part(3, 0, half), 2, self.plus))
        self.copies[1].wait_recv()
        self.copies.append(self.send(self.part(1, half, half), 3, self.minus))

    def done(self):
        self.copies[2].wait_recv()
        self.copies[3].wait_recv()

    def drain(self):
        for copy in self.copies:
            copy.wait_send()


def eye(rows, lanes):
    return lax.broadcasted_iota(jnp.int32, (rows, lanes), 0) == lax.broadcasted_iota(
        jnp.int32, (rows, lanes), 1
    )


def step_kernel(
    teacher, projection, student, gain, w_gate, w_up, w_down, row_old, col_old,
    out0, out1, out2, row_out, col_out, total_out,
    proj_v, wg_v, wu_v, wd_v, sq, sq_in, tpart, tpart_in, normed, part, mid, mid32, recv1, acc1,
    recv2, acc2, hidden, act_v, ups_v, down_acc, down_part, down_in, dy, gpart, gmid, gmid32,
    grecv1, gacc1, grecv2, gacc2, grads, big,
    left, racc, pacc, csend, cin, cfull, rsend, rin, cnew, qsend, qin, kpart, kin, kfull,
    load_sem, out_sem, sq_ss, sq_rs, t_ss, t_rs, n_ss, n_rs, d_ss, d_rs, y_ss, y_rs,
    s_ss, s_rs, g_ss, g_rs,
    c_ss, c_rs, a_ss, a_rs, r_ss, r_rs, q_ss, q_rs, k_ss, k_rs, m_ss, m_rs,
):
    me = lax.axis_index("row")
    c = lax.axis_index("col")
    x, z = lax.div(me, 4), lax.rem(me, 4)
    greet(me, c)
    loads = [
        pltpu.make_async_copy(src, dst, load_sem.at[i])
        for i, (src, dst) in enumerate(
            ((projection, proj_v), (w_gate, wg_v), (w_up, wu_v), (w_down, wd_v))
        )
    ]
    for load in loads:
        load.start()
    own = pl.ds(pl.multiple_of(c * TL, TL), TL)
    inputs = student[...].astype(F32)
    diag = eye(TL, 128)
    sums = jnp.sum(inputs * inputs, axis=1, keepdims=True)
    sq[...] = jnp.broadcast_to(
        jnp.sum(jnp.where(diag, sums, 0.0), axis=0, keepdims=True), (8, 128)
    )
    loads[0].wait()
    for i in range(4):
        product = jnp.dot(
            teacher[...], proj_v[:, i * 4 * DL : (i + 1) * 4 * DL], preferred_element_type=F32
        )
        for j in range(4):
            tpart[i * 4 + j] = product[:, j * DL : (j + 1) * DL].astype(BF16)
    met()
    sq_copies = exchange(
        "row", me, NR, lambda peer: sq, lambda d: sq_in.at[d - 1], sq_ss, sq_rs
    )
    t_copies = exchange(
        "row", me, NR, lambda peer: tpart.at[peer], lambda d: tpart_in.at[d - 1], t_ss, t_rs
    )
    for copy in sq_copies:
        copy.wait_recv()
    total = sq[0:1] + jnp.sum(sq_in[:, 0, :], axis=0, keepdims=True)
    mean_sq = jnp.sum(jnp.where(diag, total, 0.0), axis=1, keepdims=True) / D
    inv_rms = 1.0 / jnp.sqrt(mean_sq + 1e-06)
    normed[own, :] = (inputs * inv_rms * gain[...].astype(F32).reshape(1, DL)).astype(BF16)
    n_copies = exchange(
        "col", c, NC, lambda peer: normed.at[own, :], lambda d: normed.at[own, :], n_ss, n_rs
    )
    for copy in n_copies:
        copy.wait_recv()
    for load in loads[1:]:
        load.wait()

    xp, xm = lax.rem(x + 1, 4) * 4 + z, lax.rem(x + 3, 4) * 4 + z
    zp, zm = x * 4 + lax.rem(z + 1, 4), x * 4 + lax.rem(z + 3, 4)
    first = ((x, xp, xm), (z, zp, zm))
    second = ((z, zp, zm), (x, xp, xm))
    drains = []

    def owner(s):
        base = pl.multiple_of(first[s][0] * 64, 64)
        return base, pl.ds(pl.multiple_of(base + second[s][0] * 16, 16), 16)

    def tile(k):
        return slice(k * TILE, (k + 1) * TILE)

    def run(stages):
        for stage in stages:
            for j in range(3):
                for s in range(2):
                    stage(s, j)

    sc1, sc2, ga1, ga2 = {}, {}, {}, {}

    def f_start(s, j):
        k = 3 * s + j

        for weights, off in ((wg_v, 0), (wu_v, TILE)):
            value = jnp.dot(normed[...], weights[:, tile(k)], preferred_element_type=F32)
            lo = j * 2 * TILE + off
            big[s * TOKENS : (s + 1) * TOKENS, lo : lo + TILE] = value
            lo = k * 2 * TILE + off
            part[:, lo : lo + TILE] = value.astype(BF16)

        sc1[k] = Scatter(
            part, big.at[s * TOKENS : (s + 1) * TOKENS], 64, k * 2 * TILE, j * 2 * TILE, 2 * TILE,
            *first[s], recv1.at[k], acc1.at[k], s_ss.at[k], s_rs.at[k],
        )
        sc1[k].start()
        drains.append(sc1[k])

    gram = {}

    def f_gram(s, j):
        if s == 0 and j == 0:
            kpart[...] = lax.dot_general(
                normed[...], normed[...], (((1,), (1,)), ((), ())), preferred_element_type=F32
            ).astype(BF16)
            gram["sum"] = exchange(
                "row", me, NR,
                lambda peer: kpart.at[pl.ds(pl.multiple_of(peer * 16, 16), 16), :],
                lambda d: kin.at[d - 1], k_ss, k_rs,
            )

    def f_gram_all(s, j):
        if s == 0 and j == 0:
            rows = pl.ds(pl.multiple_of(me * 16, 16), 16)
            for copy in gram["sum"]:
                copy.wait_recv()
            value = kpart[rows, :].astype(F32)
            for d in range(NR - 1):
                value = value + kin[d].astype(F32)
            kfull[rows, :] = value.astype(BF16)
            gram["all"] = exchange(
                "row", me, NR, lambda peer: kfull.at[rows, :], lambda d: kfull.at[rows, :],
                m_ss, m_rs,
            )

    def f_relay1(s, j):
        sc1[3 * s + j].relay()

    def f_second(s, j):
        k = 3 * s + j
        for h, value in enumerate(sc1[k].result()):
            at = slice(h * TILE, (h + 1) * TILE)
            mid32[k, :, at] = value
            mid[k, :, at] = value.astype(BF16)
        sc2[k] = Scatter(
            mid.at[k], mid32.at[k], 16, 0, 0, 2 * TILE, *second[s], recv2.at[k], acc2.at[k],
            s_ss.at[6 + k], s_rs.at[6 + k],
        )
        sc2[k].start()
        drains.append(sc2[k])

    def f_relay2(s, j):
        sc2[3 * s + j].relay()

    def f_hidden(s, j):
        k = 3 * s + j
        gate, up = sc2[k].result()
        act, slope = gelu_pair(gate)
        act_v[k] = act
        ups_v[k] = up * slope
        base, rows = owner(s)
        hidden[rows, k * TILE : (k + 1) * TILE] = (act * up).astype(BF16)
        ga1[k] = Gather(hidden, base, 16, k * TILE, TILE, *second[s], g_ss.at[k], g_rs.at[k])
        ga1[k].start()
        drains.append(ga1[k])

    def f_relay3(s, j):
        ga1[3 * s + j].relay()

    def f_gather(s, j):
        k = 3 * s + j
        ga1[k].done()
        ga2[k] = Gather(
            hidden, 0, 64, k * TILE, TILE, *first[s], g_ss.at[6 + k], g_rs.at[6 + k]
        )
        ga2[k].start()
        drains.append(ga2[k])

    def f_relay4(s, j):
        ga2[3 * s + j].relay()

    down_acc[...] = jnp.zeros_like(down_acc)

    def f_down(s, j):
        k = 3 * s + j
        ga2[k].done()

        down_acc[...] += lax.dot_general(
            hidden[:, tile(k)], wd_v[:, tile(k)], (((1,), (1,)), ((), ())),
            preferred_element_type=F32,
        )

    run((f_start, f_gram, f_relay1, f_second, f_gram_all, f_relay2, f_hidden, f_relay3, f_gather, f_relay4, f_down))

    down_part[...] = down_acc[...].astype(BF16)
    d_copies = exchange(
        "col", c, NC,
        lambda peer: down_part.at[pl.ds(pl.multiple_of(peer * TL, TL), TL), :],
        lambda d: down_in.at[d - 1], d_ss, d_rs,
    )
    finish(t_copies)
    target = tpart[me].astype(F32)
    for d in range(NR - 1):
        target = target + tpart_in[d].astype(F32)
    rest = inputs - target.astype(BF16).astype(F32)
    for copy in d_copies:
        copy.wait_recv()
    down = down_acc[own, :]
    for d in range(NC - 1):
        down = down + down_in[d].astype(F32)
    residue = rest + down
    dy[own, :] = (residue / TOKENS).astype(BF16)
    y_copies = exchange(
        "col", c, NC, lambda peer: dy.at[own, :], lambda d: dy.at[own, :], y_ss, y_rs
    )
    rsend[...] = jnp.zeros_like(rsend) + jnp.sum(residue * residue)
    left[0] = normed[...].astype(F32).T.astype(BF16)
    for copy in y_copies:
        copy.wait_recv()

    gs1, gs2, gg1, gg2 = {}, {}, {}, {}
    half = TILE // 2
    csend[...] = jnp.zeros_like(csend)
    racc[...] = jnp.zeros_like(racc)
    pacc[...] = jnp.zeros_like(pacc)

    def b_start(s, j):
        k = 3 * s + j

        value = jnp.dot(dy[...], wd_v[:, tile(k)], preferred_element_type=F32)
        big[0:TOKENS, tile(k)] = value
        gpart[:, tile(k)] = value.astype(BF16)

        gs1[k] = Scatter(
            gpart, big.at[0:TOKENS], 64, k * TILE, k * TILE, TILE, *first[s],
            grecv1.at[k], gacc1.at[k], s_ss.at[12 + k], s_rs.at[12 + k],
        )
        gs1[k].start()
        drains.append(gs1[k])

    def b_relay1(s, j):
        gs1[3 * s + j].relay()

    def b_second(s, j):
        k = 3 * s + j
        for h, value in enumerate(gs1[k].result()):
            at = slice(h * half, (h + 1) * half)
            gmid32[k, :, at] = value
            gmid[k, :, at] = value.astype(BF16)
        gs2[k] = Scatter(
            gmid.at[k], gmid32.at[k], 16, 0, 0, TILE, *second[s], grecv2.at[k], gacc2.at[k],
            s_ss.at[18 + k], s_rs.at[18 + k],
        )
        gs2[k].start()
        drains.append(gs2[k])

    def b_relay2(s, j):
        gs2[3 * s + j].relay()

    def b_inputs(s, j):
        k = 3 * s + j
        base, rows = owner(s)
        for h, value in enumerate(gs2[k].result()):
            at = slice(h * half, (h + 1) * half)
            lo = 2 * k * TILE + h * half
            grads[rows, lo : lo + half] = (value * ups_v[k, :, at]).astype(BF16)
            lo = lo + TILE
            grads[rows, lo : lo + half] = (value * act_v[k, :, at]).astype(BF16)
        gg1[k] = Gather(
            grads, base, 16, 2 * k * TILE, 2 * TILE, *second[s], g_ss.at[12 + k], g_rs.at[12 + k]
        )
        gg1[k].start()
        drains.append(gg1[k])

    def b_relay3(s, j):
        gg1[3 * s + j].relay()

    def b_gather(s, j):
        k = 3 * s + j
        gg1[k].done()
        gg2[k] = Gather(
            grads, 0, 64, 2 * k * TILE, 2 * TILE, *first[s], g_ss.at[18 + k], g_rs.at[18 + k]
        )
        gg2[k].start()
        drains.append(gg2[k])

    def b_relay4(s, j):
        gg2[3 * s + j].relay()

    def weigh(m, k, grad):
        square = grad * grad
        folded = square[:, 0:128]
        for n in range(1, TILE // 128):
            folded = folded + square[:, n * 128 : (n + 1) * 128]
        racc[m] += folded
        return square

    def weighted(m, k, square):
        lanes = slice(k * TILE, (k + 1) * TILE)
        square = square * (1.0 / cnew[m : m + 1, lanes])
        folded = square[:, 0:128]
        for n in range(1, TILE // 128):
            folded = folded + square[:, n * 128 : (n + 1) * 128]
        pacc[m] += folded

    def b_relay1_and_down(s, j):
        k = 3 * s + j
        if k == 0:
            left[1] = dy[...].astype(F32).T.astype(BF16)
        b_relay1(s, j)
        grad = jnp.dot(left[1], hidden[:, tile(k)], preferred_element_type=F32)
        big[2 * DL : 3 * DL, tile(k)] = grad
        column = jnp.sum(weigh(2, k, grad), axis=0, keepdims=True)
        for n in range(6):
            at = k * 6 + n
            csend[at : at + 1, :] = column[:, n * 128 : (n + 1) * 128]

    cols = {}
    mine = pl.ds(pl.multiple_of(me * 8, 8), 8)

    def b_columns(s, j):
        if s == 0 and j == 0:
            cols["sum"] = exchange(
                "row", me, NR,
                lambda peer: csend.at[pl.ds(pl.multiple_of(peer * 8, 8), 8), :],
                lambda d: cin.at[d - 1], c_ss, c_rs,
            )

    def b_columns_all(s, j):
        if s == 0 and j == 0:
            for copy in cols["sum"]:
                copy.wait_recv()
            cfull[mine, :] = csend[mine, :] + jnp.sum(cin[...], axis=0)
            cols["all"] = exchange(
                "row", me, NR, lambda peer: cfull.at[mine, :], lambda d: cfull.at[mine, :],
                a_ss, a_rs,
            )

    def b_columns_use(s, j):
        if s == 0 and j == 0:
            for copy in cols["all"]:
                copy.wait_recv()
            for n in range(FL // 128):
                cnew[2:3, n * 128 : (n + 1) * 128] = cfull[n : n + 1, :]
            cnew[2:3, :] = 0.8 * col_old[2:3, :] + 0.2 * (cnew[2:3, :] / D + 1e-30)
            for copy in gram["all"]:
                copy.wait_recv()
        k = 3 * s + j
        grad = big[2 * DL : 3 * DL, tile(k)]
        weighted(2, k, grad * grad)

    def b_sums(s, j):
        k = 3 * s + j
        gg2[k].done()
        for m in range(2):
            at = slice((2 * k + m) * TILE, (2 * k + m + 1) * TILE)
            rhs = grads[:, at]
            spread = jnp.dot(kfull[...], rhs, preferred_element_type=F32)
            column = jnp.sum(spread * rhs.astype(F32), axis=0, keepdims=True)
            column = jnp.maximum(column, 0.0)
            cnew[m : m + 1, tile(k)] = 0.8 * col_old[m : m + 1, tile(k)] + 0.2 * (
                column / D + 1e-30
            )
            grad = jnp.dot(left[0], rhs, preferred_element_type=F32)
            big[m * DL : (m + 1) * DL, tile(k)] = grad
            weighted(m, k, weigh(m, k, grad))

    run(
        (
            b_start, b_relay1_and_down, b_columns, b_second, b_relay2, b_columns_all, b_inputs,
            b_relay3, b_gather, b_columns_use, b_relay4, b_sums,
        )
    )
    wide = eye(DL, DL)
    for m in range(3):
        for row, acc in ((m, racc), (3 + m, pacc)):
            sums = jnp.sum(acc[m], axis=1, keepdims=True)
            rsend[row : row + 1, :] = jnp.sum(
                jnp.where(wide, sums, 0.0), axis=0, keepdims=True
            )
    r_copies = exchange(
        "col", c, NC, lambda peer: rsend, lambda d: rin.at[d - 1], r_ss, r_rs
    )
    col_out[...] = cnew[...]
    cnew[...] = 1.0 / jnp.sqrt(cnew[...])
    for copy in r_copies:
        copy.wait_recv()
    row_sum = rsend[...] + jnp.sum(rin[...], axis=0)
    row_new = 0.8 * row_old[...] + 0.2 * (row_sum[0:3] / FF + 1e-30)
    row_out[...] = row_new
    qsend[0:3, :] = jnp.broadcast_to(
        jnp.sum(row_sum[3:6] / row_new, axis=1, keepdims=True), (3, 128)
    )
    qsend[3:8, :] = jnp.broadcast_to(row_sum[6:7, 0:1], (5, 128))
    q_copies = exchange(
        "row", me, NR, lambda peer: qsend, lambda d: qin.at[d - 1], q_ss, q_rs
    )
    scale = 1.0 / jnp.sqrt(row_new)
    out_copies = []
    for m, (staged, out) in enumerate(((wg_v, out0), (wu_v, out1), (wd_v, out2))):
        racc[m] = jnp.broadcast_to(
            jnp.sum(jnp.where(wide, scale[m : m + 1], 0.0), axis=1, keepdims=True), (DL, 128)
        )

        @pl.loop(0, FL // 256)
        def _(i):
            for n in range(2):
                lanes = pl.ds(pl.multiple_of(i * 256 + n * 128, 128), 128)
                staged[:, lanes] = (
                    big[m * DL : (m + 1) * DL, lanes] * racc[m] * cnew[m : m + 1, lanes]
                ).astype(BF16)

        copy = pltpu.make_async_copy(staged, out, out_sem.at[m])
        copy.start()
        out_copies.append(copy)
    for copy in q_copies:
        copy.wait_recv()
    total_out[...] = qsend[...] + jnp.sum(qin[...], axis=0)
    for copy in sq_copies + n_copies + d_copies + y_copies + gram["sum"] + gram["all"]:
        copy.wait_send()
    for copy in cols["sum"] + cols["all"] + r_copies + q_copies:
        copy.wait_send()
    for one in drains:
        one.drain()
    for copy in out_copies:
        copy.wait()


def whole(space=pltpu.VMEM):
    return pl.BlockSpec(memory_space=space)


def step(teacher, projection, student, gain, w_gate, w_up, w_down, row_old, col_old):
    sem = pltpu.SemaphoreType.DMA
    half = TILE // 2
    return pl.pallas_call(
        step_kernel,
        out_shape=(
            jax.ShapeDtypeStruct((DL, FL), BF16),
            jax.ShapeDtypeStruct((DL, FL), BF16),
            jax.ShapeDtypeStruct((DL, FL), BF16),
            jax.ShapeDtypeStruct((3, DL), F32),
            jax.ShapeDtypeStruct((3, FL), F32),
            jax.ShapeDtypeStruct((8, 128), F32),
        ),
        in_specs=[
            whole(), whole(pl.ANY), whole(), whole(), whole(pl.ANY), whole(pl.ANY), whole(pl.ANY),
            whole(), whole(),
        ],
        out_specs=(whole(pl.ANY),) * 3 + (whole(),) * 3,
        scratch_shapes=[
            pltpu.VMEM(projection.shape, BF16),
            pltpu.VMEM((DL, FL), BF16),
            pltpu.VMEM((DL, FL), BF16),
            pltpu.VMEM((DL, FL), BF16),
            pltpu.VMEM((8, 128), F32),
            pltpu.VMEM((NR - 1, 8, 128), F32),
            pltpu.VMEM((NR, TL, DL), BF16),
            pltpu.VMEM((NR - 1, TL, DL), BF16),
            pltpu.VMEM((TOKENS, DL), BF16),
            pltpu.VMEM((TOKENS, 2 * FL), BF16),
            pltpu.VMEM((6, 64, 2 * TILE), BF16),
            pltpu.VMEM((6, 64, 2 * TILE), F32),
            pltpu.VMEM((6, 6, 64, TILE), BF16),
            pltpu.VMEM((6, 2, 64, TILE), BF16),
            pltpu.VMEM((6, 6, 16, TILE), BF16),
            pltpu.VMEM((6, 2, 16, TILE), BF16),
            pltpu.VMEM((TOKENS, FL), BF16),
            pltpu.VMEM((6, 16, TILE), F32),
            pltpu.VMEM((6, 16, TILE), F32),
            pltpu.VMEM((TOKENS, DL), F32),
            pltpu.VMEM((TOKENS, DL), BF16),
            pltpu.VMEM((NC - 1, TL, DL), BF16),
            pltpu.VMEM((TOKENS, DL), BF16),
            pltpu.VMEM((TOKENS, FL), BF16),
            pltpu.VMEM((6, 64, TILE), BF16),
            pltpu.VMEM((6, 64, TILE), F32),
            pltpu.VMEM((6, 6, 64, half), BF16),
            pltpu.VMEM((6, 2, 64, half), BF16),
            pltpu.VMEM((6, 6, 16, half), BF16),
            pltpu.VMEM((6, 2, 16, half), BF16),
            pltpu.VMEM((TOKENS, 2 * FL), BF16),
            pltpu.VMEM((3 * DL, FL), F32),
            pltpu.VMEM((2, DL, TOKENS), BF16),
            pltpu.VMEM((3, DL, 128), F32),
            pltpu.VMEM((3, DL, 128), F32),
            pltpu.VMEM((128, 128), F32),
            pltpu.VMEM((NR - 1, 8, 128), F32),
            pltpu.VMEM((128, 128), F32),
            pltpu.VMEM((8, DL), F32),
            pltpu.VMEM((NC - 1, 8, DL), F32),
            pltpu.VMEM((3, FL), F32),
            pltpu.VMEM((8, 128), F32),
            pltpu.VMEM((NR - 1, 8, 128), F32),
            pltpu.VMEM((TOKENS, TOKENS), BF16),
            pltpu.VMEM((NR - 1, 16, TOKENS), BF16),
            pltpu.VMEM((TOKENS, TOKENS), BF16),
            sem((4,)), sem((4,)),
            sem((NR - 1,)), sem((NR - 1,)), sem((NR - 1,)), sem((NR - 1,)),
            sem((NC - 1,)), sem((NC - 1,)), sem((NC - 1,)), sem((NC - 1,)),
            sem((NC - 1,)), sem((NC - 1,)),
            sem((24, 6)), sem((24, 6)), sem((24, 4)), sem((24, 4)),
            sem((NR - 1,)), sem((NR - 1,)), sem((NR - 1,)), sem((NR - 1,)),
            sem((NC - 1,)), sem((NC - 1,)), sem((NR - 1,)), sem((NR - 1,)),
            sem((NR - 1,)), sem((NR - 1,)), sem((NR - 1,)), sem((NR - 1,)),
        ],
        compiler_params=pltpu.CompilerParams(
            collective_id=0, has_side_effects=True, vmem_limit_bytes=VMEM_LIMIT
        ),
        name="step",
    )(teacher, projection, student, gain, w_gate, w_up, w_down, row_old, col_old)


def clip_kernel(total, in0, in1, in2, out0, out1, out2):
    for m, (value, out) in enumerate(((in0, out0), (in1, out1), (in2, out2))):
        mean = total[m : m + 1, :] / (float(D) * FF)
        clip = 1.0 / jnp.maximum(1.0, jnp.sqrt(mean))
        for k in range(TILE // 128):
            at = slice(k * 128, (k + 1) * 128)
            out[:, at] = (value[:, at].astype(F32) * clip).astype(BF16)


def clipped(total, values):
    tile = pl.BlockSpec((DL, TILE), lambda i: (0, i))
    return pl.pallas_call(
        clip_kernel,
        grid=(FL // TILE,),
        out_shape=(jax.ShapeDtypeStruct((DL, FL), BF16),) * 3,
        in_specs=[pl.BlockSpec((8, 128), lambda i: (0, 0)), tile, tile, tile],
        out_specs=(tile,) * 3,
        compiler_params=pltpu.CompilerParams(dimension_semantics=("arbitrary",)),
        name="clip",
    )(total, *values)


def shards(teacher_rows, projection, student_in, norm_gain, w_gate, w_up, w_down, row_old, col_old):
    *values, row_new, col_new, total = step(
        teacher_rows, projection, student_in, norm_gain, w_gate, w_up, w_down,
        row_old, col_old,
    )
    out = clipped(total, values)
    return (*out, row_new, col_new, 0.5 * total[3, 0] / TOKENS)


def solution(mesh):
    placed = (
        P("col", "row"),
        P("row", None),
        P("col", "row"),
        P("row"),
        P("row", "col"),
        P("row", "col"),
        P("row", "col"),
        P(None, "row"),
        P(None, "col"),
    )
    return jax.shard_map(
        shards,
        mesh=mesh,
        in_specs=placed,
        out_specs=(
            P("row", "col"),
            P("row", "col"),
            P("row", "col"),
            P(None, "row"),
            P(None, "col"),
            P(),
        ),
        check_vma=False,
    )
```
